32 devices in a mesh: blk: 16 (over z, x, core), tp: 2 (over y).
Axes of the slice: x: 2, y: 2, z: 4, core: 2. Of those that a mesh axis runs over, the one named last changes fastest.
Arguments:
- inputs: bfloat16 [2048, 8192], P('blk', 'tp'), may hold values from -6 to 6
- grad_out: bfloat16 [2048, 8192], P('blk', 'tp'), may hold values from -6 to 6
- w_up: bfloat16 [32, 2, 128, 128], P('blk'), may hold values from -0.4375 to 0.4375
- w_down: bfloat16 [32, 2, 128, 128], P('blk'), may hold values from -0.625 to 0.625
- up_rows: int32 [32, 2], P('blk'), may hold values from 0 to 63, as said below
- slot_counts: int32 [32], P('blk'), may hold values from 1 to 2
- keep_mask: int32 [2048, 256], P(None, 'blk'), may hold values from 0 to 65535, as said below
Outputs:
- outputs: bfloat16 [2048, 8192], P('blk', 'tp')
- grad_in: bfloat16 [2048, 8192], P('blk', 'tp')
- grad_up: bfloat16 [32, 2, 128, 128], P('blk', None, 'tp')
- grad_down: bfloat16 [32, 2, 128, 128], P('blk', None, 'tp')
The draws below stay inside these ranges and needn't reach their ends.
Inputs may be any that keep to these rules, and one draw needn't show every extreme that they name: `up_rows`: within each hidden column block, the 2 entries are distinct. `keep_mask`: bit k of word w holds the keep flag of hidden unit 16 w + k.
All inputs are finite; a program needn't handle non-finite values.
Results may differ from the reference program's by a relative error of at most 0.005.
Values may be sent and summed in bfloat16 or wider, within the bound.
No kernel may reach another device: no remote copies, remote signals or barrier semaphores. Data moves between devices by JAX's collectives and lax.ppermute only.
A program may use at most 64 MiB of HBM per device.

```python
import jax
import jax.numpy as jnp
from jax import lax

D = 8192
TILE = 128
SLOTS = 2
TOKENS = 2048
COL_BLOCKS = 32
FF = 4096


def draw_up_rows(key, part):
    row_total = D // TILE
    scores = jax.random.randint(key, (COL_BLOCKS, row_total), 0, 1 << 20)
    scores = scores * row_total + jnp.arange(row_total, dtype=jnp.int32)
    order = jnp.argsort(scores, axis=-1)
    return order[:, :SLOTS].astype(jnp.int32)


def draw_keep_mask(key, part):
    flags = (jax.random.randint(key, (TOKENS, FF // 16, 16), 0, 5) > 0).astype(jnp.int32)
    powers = jnp.left_shift(jnp.ones((16,), jnp.int32), jnp.arange(16, dtype=jnp.int32))
    return jnp.sum(flags * powers, axis=-1).astype(jnp.int32)


def touch_ends(entries, own_key, smallest, high):
    longest = entries.shape.index(max(entries.shape))
    spots = []
    for shift in (0, 1):
        where = [jax.random.randint(jax.random.fold_in(own_key, axis), (), 0, length) for axis, length in enumerate(entries.shape)]
        where[longest] = (where[longest] + shift) % entries.shape[longest]
        spots.append(tuple(where))
    return entries.at[spots[0]].set(smallest).at[spots[1]].set(high)


def block_scale(key, extent, cuts, smallest, top_value):
    factor_of = 1.0
    for position, shards_of in cuts:
        draws = jax.random.uniform(jax.random.fold_in(jax.random.fold_in(key, 6), position), (shards_of,), jnp.float32, smallest / len(cuts), top_value / len(cuts))
        factor_of = factor_of * jnp.repeat(jnp.exp(draws), extent[position] // shards_of).reshape((-1,) + (1,) * (len(extent) - 1 - position))
    return factor_of


def gaussian(own_key, extent, scale, limit, pieces=(), kind=jnp.bfloat16):
    drawn = scale * jax.random.normal(own_key, extent, jnp.float32)
    if pieces:
        drawn = drawn * block_scale(own_key, extent, pieces, -0.22, 0.18)
    return jnp.clip(drawn, -limit, limit).astype(kind)


def setup_inputs(seed: int = 0) -> dict:
    keys = jax.random.split(jax.random.key(seed), 8)
    return {
        "inputs": gaussian(keys[0], (TOKENS, D), 1.0, 6.0, ((0, 16), (1, 2))),
        "grad_out": gaussian(keys[1], (TOKENS, D), 1.0, 6.0, ((0, 16), (1, 2))),
        "w_up": gaussian(keys[2], (COL_BLOCKS, SLOTS, TILE, TILE), ((SLOTS + 1) * TILE // 2) ** -0.5, 0.4375, ((0, 16),)),
        "w_down": gaussian(keys[3], (COL_BLOCKS, SLOTS, TILE, TILE), (COL_BLOCKS * (SLOTS + 1) * TILE // (2 * (D // TILE))) ** -0.5, 0.625, ((0, 16),)),
        "up_rows": draw_up_rows(jax.random.fold_in(keys[7], 71), 0),
        "slot_counts": touch_ends(jax.random.randint(keys[5], (COL_BLOCKS,), 1, SLOTS + 1), jax.random.fold_in(keys[5], 1), 1, SLOTS).astype(jnp.int32),
        "keep_mask": draw_keep_mask(jax.random.fold_in(keys[7], 71), 0),
    }


INV_ROOT_TWO = 0.7071067811865476
INV_ROOT_TAU = 0.3989422804014327
KEEP_SCALE = 1.25


def gelu_value(value):
    return 0.5 * value * (1.0 + jax.scipy.special.erf(value * INV_ROOT_TWO))


def gelu_slope(value):
    return 0.5 * (1.0 + jax.scipy.special.erf(value * INV_ROOT_TWO)) + value * jnp.exp(-0.5 * value * value) * INV_ROOT_TAU


def reference(inputs, grad_out, w_up, w_down, up_rows, slot_counts, keep_mask):
    row_total = D // TILE
    slot_index = jnp.arange(SLOTS, dtype=jnp.int32)
    column = jnp.arange(TILE, dtype=jnp.int32)
    input_blocks = inputs.reshape(TOKENS, row_total, TILE)
    cotangent_blocks = grad_out.reshape(TOKENS, row_total, TILE)
    block_ids = jnp.arange(COL_BLOCKS, dtype=jnp.int32)

    def one_block(carry, items):
        out_acc, grad_acc = carry
        up_tiles, down_tiles, rows, count, block = items
        rows = rows.astype(jnp.int32)
        live = (slot_index < count).astype(jnp.float32)
        up_live = up_tiles.astype(jnp.float32) * live[:, None, None]
        down_live = down_tiles.astype(jnp.float32) * live[:, None, None]
        hidden_cols = (block * TILE + column).astype(jnp.int32)
        words = jnp.take(keep_mask, hidden_cols // 16, axis=1)
        keep = jnp.bitwise_and(jnp.right_shift(words, hidden_cols % 16), 1)
        scale = keep.astype(jnp.float32) * KEEP_SCALE
        input_tiles = jnp.take(input_blocks, rows, axis=1).astype(jnp.float32)
        cotangent_tiles = jnp.take(cotangent_blocks, rows, axis=1).astype(jnp.float32)
        pre = jnp.einsum("nsi,sij->nj", input_tiles, up_live)
        hidden = (gelu_value(pre) * scale).astype(jnp.bfloat16)
        hidden_wide = hidden.astype(jnp.float32)
        out_terms = jnp.einsum("nj,sjk->nsk", hidden_wide, down_live)
        out_acc = out_acc.at[:, rows, :].add(out_terms)
        grad_hidden = jnp.einsum("nsk,sjk->nj", cotangent_tiles, down_live)
        grad_pre = (grad_hidden * scale * gelu_slope(pre)).astype(jnp.bfloat16)
        grad_wide = grad_pre.astype(jnp.float32)
        grad_terms = jnp.einsum("nj,sij->nsi", grad_wide, up_live)
        grad_acc = grad_acc.at[:, rows, :].add(grad_terms)
        up_grad = (jnp.einsum("nsi,nj->sij", input_tiles, grad_wide) * live[:, None, None]).astype(jnp.bfloat16)
        down_grad = (jnp.einsum("nj,nsk->sjk", hidden_wide, cotangent_tiles) * live[:, None, None]).astype(jnp.bfloat16)
        return (out_acc, grad_acc), (up_grad, down_grad)

    start = (jnp.zeros((TOKENS, row_total, TILE), jnp.float32), jnp.zeros((TOKENS, row_total, TILE), jnp.float32))
    (out_acc, grad_acc), (grad_up, grad_down) = lax.scan(one_block, start, (w_up, w_down, up_rows, slot_counts, block_ids))
    outputs = out_acc.reshape(TOKENS, D).astype(jnp.bfloat16)
    grad_in = grad_acc.reshape(TOKENS, D).astype(jnp.bfloat16)
    return (outputs, grad_in, grad_up, grad_down)
```

```python
import functools

import jax
import jax.numpy as jnp
from jax import lax
from jax.experimental import pallas as pl
from jax.experimental.pallas import tpu as pltpu
from jax.sharding import PartitionSpec as P

INV_ROOT_TWO = 0.7071067811865476
INV_ROOT_TAU = 0.3989422804014327
KEEP_SCALE = 1.25
F32 = jnp.float32
BF16 = jnp.bfloat16


def mm(a, b, dims):
    return lax.dot_general(a, b, (dims, ((), ())), preferred_element_type=F32)


def ffn_kernel(first, last, count, shape, tab_ref, scale_ref, *refs):
    parts, part_rows, width_local, col_local, slots, tile = shape
    refs = list(refs)

    def take(number):
        out = refs[:number]
        del refs[:number]
        return out

    x_hbm = take(parts)
    dy_hbm = take(parts)
    up_hbm = take(count)
    down_hbm = take(count)
    acc_in = [] if first else take(2)
    if last:
        out_refs = take(parts)
        gin_refs = take(parts)
        acc_out = []
    else:
        out_refs = gin_refs = []
        acc_out = take(2)
    gup_ref, gdown_ref = take(2)
    x_s, dy_s, up_s, down_s, sems = take(5)
    out_acc, gin_acc = take(2) if last else acc_out

    me = tab_ref[count, 0]
    copies = []

    def begin(src, dst):
        copy = pltpu.make_async_copy(src, dst, sems.at[len(copies)])
        copy.start()
        copies.append(copy)

    for array, store in ((x_hbm, x_s), (dy_hbm, dy_s)):
        start = pl.multiple_of(me * part_rows, part_rows)
        begin(array[0].at[pl.ds(start, part_rows), :], store.at[me])
        for k in range(1, parts):
            begin(array[k], store.at[lax.rem(me + parts - k, parts)])
    for k in range(count):
        begin(up_hbm[k], up_s.at[k])
        begin(down_hbm[k], down_s.at[k])
    if first:
        out_acc[...] = jnp.zeros_like(out_acc)
        gin_acc[...] = jnp.zeros_like(gin_acc)
    else:
        out_acc[...] = acc_in[0][...]
        gin_acc[...] = acc_in[1][...]
    for copy in copies:
        copy.wait()

    row_local = width_local // tile

    def body(k, carry):
        pos = tab_ref[k, col_local * slots]
        for c in range(col_local):
            scale = scale_ref[pos, :, c * tile : (c + 1) * tile].astype(F32)
            where = []
            for s in range(slots):
                row = tab_ref[k, c * slots + s]
                part = lax.div(row, row_local)
                lane = pl.multiple_of(lax.rem(row, row_local) * tile, tile)
                where.append((part, lane))
            xs = [x_s[p, :, pl.ds(o, tile)] for p, o in where]
            dys = [dy_s[p, :, pl.ds(o, tile)] for p, o in where]
            ups = [up_s[k, c, s] for s in range(slots)]
            downs = [down_s[k, c, s] for s in range(slots)]
            pre = mm(xs[0], ups[0], ((1,), (0,)))
            grad_hidden = mm(dys[0], downs[0], ((1,), (1,)))
            for s in range(1, slots):
                pre += mm(xs[s], ups[s], ((1,), (0,)))
                grad_hidden += mm(dys[s], downs[s], ((1,), (1,)))
            phi = 0.5 * (1.0 + lax.erf(pre * INV_ROOT_TWO))
            slope = phi + pre * jnp.exp(-0.5 * pre * pre) * INV_ROOT_TAU
            hidden = (pre * phi * scale).astype(BF16)
            grad_pre = (grad_hidden * scale * slope).astype(BF16)
            for s, (p, o) in enumerate(where):
                out_acc[p, :, pl.ds(o, tile)] += mm(hidden, downs[s], ((1,), (0,)))
                gin_acc[p, :, pl.ds(o, tile)] += mm(grad_pre, ups[s], ((1,), (1,)))
                gup_ref[k, c, s] = mm(xs[s], grad_pre, ((0,), (0,))).astype(BF16)
                gdown_ref[k, c, s] = mm(hidden, dys[s], ((0,), (0,))).astype(BF16)
        return carry

    lax.fori_loop(0, count, body, 0)
    if last:
        for acc, outs in ((out_acc, out_refs), (gin_acc, gin_refs)):
            for k in range(parts):
                outs[k][...] = acc[lax.rem(me + k, parts)].astype(BF16)


def run_ffn(first, last, table, scale, xs, dys, ups, downs, acc, shape):
    parts, part_rows, width_local, col_local, slots, tile = shape
    count = len(ups)
    anywhere = pl.BlockSpec(memory_space=pl.ANY)
    vmem = pl.BlockSpec(memory_space=pltpu.VMEM)
    smem = pl.BlockSpec(memory_space=pltpu.SMEM)
    acc_shape = jax.ShapeDtypeStruct((parts, part_rows, width_local), F32)
    part_shape = jax.ShapeDtypeStruct((part_rows, width_local), BF16)
    grad_shape = jax.ShapeDtypeStruct((count, col_local, slots, tile, tile), BF16)
    outs = [part_shape] * (2 * parts) if last else [acc_shape] * 2
    scratch = [
        pltpu.VMEM((parts, part_rows, width_local), BF16),
        pltpu.VMEM((parts, part_rows, width_local), BF16),
        pltpu.VMEM((count, col_local, slots, tile, tile), BF16),
        pltpu.VMEM((count, col_local, slots, tile, tile), BF16),
        pltpu.SemaphoreType.DMA((2 * parts + 2 * count,)),
    ]
    if last:
        scratch += [pltpu.VMEM(acc_shape.shape, F32)] * 2
    operands = [*xs, *dys, *ups, *downs]
    result = pl.pallas_call(
        functools.partial(ffn_kernel, first, last, count, shape),
        out_shape=(*outs, grad_shape, grad_shape),
        in_specs=[smem, vmem] + [anywhere] * len(operands) + [vmem] * len(acc),
        out_specs=tuple([vmem] * (len(outs) + 2)),
        scratch_shapes=scratch,
        compiler_params=pltpu.CompilerParams(vmem_limit_bytes=60 * 1024 * 1024),
        cost_estimate=pl.CostEstimate(
            flops=12 * count * col_local * slots * tile * tile * part_rows,
            bytes_accessed=16 * 1024 * 1024,
            transcendentals=0,
        ),
    )(table, scale, *operands, *acc)
    return result[:-2], result[-2], result[-1]


def per_device(inputs, grad_out, w_up, w_down, up_rows, slot_counts, keep_mask):
    tok_dev, width_local = inputs.shape
    col_local, slots, tile, _unused = w_up.shape
    parts = lax.axis_size("tp")
    blocks = lax.axis_size("blk")
    part_rows = tok_dev // parts
    chips = blocks // 2
    half = chips // 2
    shape = (parts, part_rows, width_local, col_local, slots, tile)
    tp = lax.axis_index("tp")
    blk = lax.axis_index("blk")

    def chip_at(pos):
        return 2 * pos if pos < half else 2 * (chips - 1 - pos) + 1

    chip, core = blk // 2, blk % 2
    ring_pos = jnp.where(chip % 2 == 0, chip // 2, chips - 1 - chip // 2)
    right, left = [], []
    for pos in range(chips):
        a, b = chip_at(pos), chip_at((pos + 1) % chips)
        for c in range(2):
            right.append((2 * a + c, 2 * b + c))
            left.append((2 * b + c, 2 * a + c))
    swap = [(i, i ^ 1) for i in range(blocks)]

    def go_right(x):
        return lax.ppermute(x, "blk", right)

    def go_left(x):
        return lax.ppermute(x, "blk", left)

    def to_core(x):
        return lax.ppermute(x, "blk", swap)

    word_count = keep_mask.shape[1]
    lanes = 128
    word_rows = part_rows * word_count // lanes
    words = keep_mask.reshape(blocks, parts, word_rows * lanes)
    words = lax.dynamic_index_in_dim(words, tp, 1, keepdims=False)
    words = words.reshape(blocks, word_rows, lanes)
    flat_rows = jnp.pad(up_rows.reshape(1, -1), ((0, 0), (0, lanes - col_local * slots)))
    relative = jnp.arange(blocks, dtype=jnp.int32)
    message = jnp.concatenate(
        [
            jnp.take(words, relative ^ blk, axis=0),
            jnp.broadcast_to(flat_rows[None], (blocks, 1, lanes)),
        ],
        axis=1,
    )
    bits = blocks.bit_length() - 1
    for bit in range(bits):
        split = message.reshape(blocks >> (bit + 1), 2, 1 << bit, word_rows + 1, lanes)
        pairs = [(i, i ^ (1 << bit)) for i in range(blocks)]
        moved = lax.ppermute(split[:, 1], "blk", pairs)
        message = jnp.stack([split[:, 0], moved], axis=1).reshape(blocks, word_rows + 1, lanes)

    def to_tokens(x):
        pieces = [x]
        for k in range(1, parts):
            dest = lax.rem(tp + k, parts)
            piece = lax.dynamic_slice_in_dim(x, dest * part_rows, part_rows, 0)
            pieces.append(lax.ppermute(piece, "tp", [(i, (i + k) % parts) for i in range(parts)]))
        return pieces

    xs = to_tokens(inputs)
    dys = to_tokens(grad_out)

    live = jnp.arange(slots, dtype=jnp.int32)[None, :] < slot_counts[:, None]
    live_tiles = live[:, :, None, None]
    up = {0: jnp.where(live_tiles, w_up, jnp.zeros((), BF16))}
    down = {0: jnp.where(live_tiles, w_down, jnp.zeros((), BF16))}
    for step in range(1, half):
        for w in (up, down):
            w[-step] = go_right(w[1 - step])
            w[step] = go_left(w[step - 1])
    up[half] = go_right(up[1 - half])
    down[half] = go_left(down[half - 1])
    order = [half]
    for step in range(half - 1, 0, -1):
        order += [step, -step]
    order.append(0)
    up_other = [to_core(up[d]) for d in order]
    down_other = [to_core(down[d]) for d in order]
    up_mine = [up[d] for d in order]
    down_mine = [down[d] for d in order]

    owner_pos = lax.rem(ring_pos + jnp.asarray(order, jnp.int32) + chips, chips)
    owner_chip = jnp.where(owner_pos < half, 2 * owner_pos, 2 * (chips - 1 - owner_pos) + 1)
    rows_by_rel = message[:, word_rows, : col_local * slots]

    def table_for(owner_core):
        rel = (2 * owner_chip + owner_core) ^ blk
        tab = jnp.concatenate([jnp.take(rows_by_rel, rel, axis=0), rel[:, None]], axis=1)
        return jnp.concatenate([tab, jnp.full((1, tab.shape[1]), tp, jnp.int32)], axis=0)

    columns = jnp.arange(col_local * tile, dtype=jnp.int32)
    mine = message[:, :word_rows].reshape(blocks * part_rows, word_count)
    picked = jnp.take(mine, columns // 16, axis=1)
    keep = jnp.bitwise_and(jnp.right_shift(picked, columns % 16), 1)
    scale = (keep.astype(F32) * KEEP_SCALE).astype(BF16)
    scale = scale.reshape(blocks, part_rows, col_local * tile)

    acc, gup_other, gdown_other = run_ffn(
        True, False, table_for(1 - core), scale, xs, dys, up_other, down_other, (), shape
    )
    gup_moved, gdown_moved = to_core(gup_other), to_core(gdown_other)
    pieces, gup, gdown = run_ffn(
        False, True, table_for(core), scale, xs, dys, up_mine, down_mine, acc, shape
    )

    def to_width(pieces):
        arrived = [pieces[0]]
        for k in range(1, parts):
            arrived.append(lax.ppermute(pieces[k], "tp", [(i, (i + k) % parts) for i in range(parts)]))
        stacked = jnp.stack(arrived)
        place = lax.rem(tp + parts - jnp.arange(parts, dtype=jnp.int32), parts)
        return jnp.take(stacked, place, axis=0).reshape(tok_dev, width_local)

    outputs = to_width(pieces[:parts])
    grad_in = to_width(pieces[parts:])

    def reduce_ring(mine, other, first_right):
        term = {
            d: mine[i].astype(F32) + other[i].astype(F32) for i, d in enumerate(order)
        }
        moving_right = go_right(term[half].astype(BF16)) if first_right else None
        moving_left = None if first_right else go_left(term[half].astype(BF16))
        for step in range(half - 1, 0, -1):
            r, l = term[step], term[-step]
            if moving_right is not None:
                r = r + moving_right.astype(F32)
            if moving_left is not None:
                l = l + moving_left.astype(F32)
            moving_right = go_right(r.astype(BF16))
            moving_left = go_left(l.astype(BF16))
        total = term[0]
        for part in (moving_right, moving_left):
            if part is not None:
                total = total + part.astype(F32)
        return total

    def reduce_tp(total):
        rows = tile // parts
        out = lax.dynamic_slice_in_dim(total, tp * rows, rows, 2)
        for k in range(1, parts):
            dest = lax.rem(tp + k, parts)
            piece = lax.dynamic_slice_in_dim(total, dest * rows, rows, 2).astype(BF16)
            moved = lax.ppermute(piece, "tp", [(i, (i + k) % parts) for i in range(parts)])
            out = out + moved.astype(F32)
        return jnp.where(live_tiles, out, 0.0).astype(BF16)

    grad_up = reduce_tp(reduce_ring(gup, gup_moved, True))
    grad_down = reduce_tp(reduce_ring(gdown, gdown_moved, False))
    return (outputs, grad_in, grad_up, grad_down)


def solution(mesh):
    return jax.shard_map(
        per_device,
        mesh=mesh,
        in_specs=(
            P("blk", "tp"),
            P("blk", "tp"),
            P("blk", None, None, None),
            P("blk", None, None, None),
            P("blk", None),
            P("blk"),
            P(None, "blk"),
        ),
        out_specs=(
            P("blk", "tp"),
            P("blk", "tp"),
            P("blk", None, "tp", None),
            P("blk", None, "tp", None),
        ),
        check_vma=False,
    )
```

```python
import functools

import jax
import jax.numpy as jnp
from jax import lax
from jax.experimental import pallas as pl
from jax.experimental.pallas import tpu as pltpu
from jax.sharding import PartitionSpec as P

INV_ROOT_TWO = 0.7071067811865476
INV_ROOT_TAU = 0.3989422804014327
KEEP_SCALE = 1.25
F32 = jnp.float32
BF16 = jnp.bfloat16


def mm(a, b, dims):
    return lax.dot_general(a, b, (dims, ((), ())), preferred_element_type=F32)


def ffn_kernel(count, shape, tab_ref, scale_ref, *refs):
    cores, parts, part_rows, width_local, col_local, slots, tile = shape
    tokens = cores * part_rows
    refs = list(refs)

    def take(number):
        out = refs[:number]
        del refs[:number]
        return out

    x_hbm = take(cores * parts)
    dy_hbm = take(cores * parts)
    up_hbm = take(count)
    down_hbm = take(count)
    outs = take(cores)
    gins = take(cores)
    gup_ref, gdown_ref = take(2)
    x_s, dy_s, out_acc, gin_acc, up_s, down_s, sems = take(7)

    me = tab_ref[count, 0]
    copies = []

    def begin(src, dst):
        copy = pltpu.make_async_copy(src, dst, sems.at[len(copies)])
        copy.start()
        copies.append(copy)

    for array, store in ((x_hbm, x_s), (dy_hbm, dy_s)):
        for core in range(cores):
            for k in range(parts):
                src = array[core * parts + k]
                if core == 0 and k == 0:
                    src = src.at[pl.ds(pl.multiple_of(me * part_rows, part_rows), part_rows), :]
                at = pl.ds(core * part_rows, part_rows)
                begin(src, store.at[lax.rem(me + parts - k, parts), at, :])
    for k in range(count):
        begin(up_hbm[k], up_s.at[k])
        begin(down_hbm[k], down_s.at[k])
    out_acc[...] = jnp.zeros_like(out_acc)
    gin_acc[...] = jnp.zeros_like(gin_acc)
    for copy in copies:
        copy.wait()

    row_local = width_local // tile
    per_step = 2 if count % 2 == 0 else 1

    def body(step, carry):
        items = []
        for sub in range(per_step):
            k = step * per_step + sub
            pos = tab_ref[k, col_local * (slots + 1)]
            for c in range(col_local):
                lives = tab_ref[k, col_local * slots + c]
                where, xs, dys, ups, downs = [], [], [], [], []
                for s in range(slots):
                    row = tab_ref[k, c * slots + s]
                    part = lax.div(row, row_local)
                    lane = pl.multiple_of(lax.rem(row, row_local) * tile, tile)
                    where.append((part, lane))
                    xs.append(x_s[part, :, pl.ds(lane, tile)])
                    dys.append(dy_s[part, :, pl.ds(lane, tile)])
                    zero = jnp.zeros((tile, tile), BF16)
                    ups.append(jnp.where(s < lives, up_s[k, c, s], zero))
                    downs.append(jnp.where(s < lives, down_s[k, c, s], zero))
                pre = mm(xs[0], ups[0], ((1,), (0,)))
                grad_hidden = mm(dys[0], downs[0], ((1,), (1,)))
                for s in range(1, slots):
                    pre += mm(xs[s], ups[s], ((1,), (0,)))
                    grad_hidden += mm(dys[s], downs[s], ((1,), (1,)))
                items.append((k, c, pos, where, xs, dys, ups, downs, pre, grad_hidden))
        ready = []
        for k, c, pos, where, xs, dys, ups, downs, pre, grad_hidden in items:
            scale = scale_ref[pos, :, c * tile : (c + 1) * tile].astype(F32)
            phi = 0.5 * (1.0 + lax.erf(pre * INV_ROOT_TWO))
            slope = phi + pre * jnp.exp(-0.5 * pre * pre) * INV_ROOT_TAU
            hidden = (pre * phi * scale).astype(BF16)
            grad_pre = (grad_hidden * scale * slope).astype(BF16)
            ready.append((k, c, where, xs, dys, ups, downs, hidden, grad_pre))
        for k, c, where, xs, dys, ups, downs, hidden, grad_pre in ready:
            for s in range(slots):
                gup_ref[k, c, s] = mm(xs[s], grad_pre, ((0,), (0,)))
                gdown_ref[k, c, s] = mm(hidden, dys[s], ((0,), (0,)))
        for k, c, where, xs, dys, ups, downs, hidden, grad_pre in ready:
            for s, (p, o) in enumerate(where):
                out_acc[p, :, pl.ds(o, tile)] += mm(hidden, downs[s], ((1,), (0,)))
                gin_acc[p, :, pl.ds(o, tile)] += mm(grad_pre, ups[s], ((1,), (1,)))
        return carry

    lax.fori_loop(0, count // per_step, body, 0)
    for acc, results in ((out_acc, outs), (gin_acc, gins)):
        for core in range(cores):
            value = acc[:, core * part_rows : (core + 1) * part_rows, :]
            results[core][...] = value.astype(results[core].dtype)


def run_ffn(table, scale, xs, dys, ups, downs, shape):
    cores, parts, part_rows, width_local, col_local, slots, tile = shape
    count = len(ups)
    anywhere = pl.BlockSpec(memory_space=pl.ANY)
    vmem = pl.BlockSpec(memory_space=pltpu.VMEM)
    smem = pl.BlockSpec(memory_space=pltpu.SMEM)
    own_shape = jax.ShapeDtypeStruct((parts, part_rows, width_local), F32)
    other_shape = jax.ShapeDtypeStruct((parts, part_rows, width_local), BF16)
    grad_shape = jax.ShapeDtypeStruct((count, col_local, slots, tile, tile), F32)
    outs = [own_shape] + [other_shape] * (cores - 1)
    token_shape = (parts, cores * part_rows, width_local)
    operands = [*xs, *dys, *ups, *downs]
    result = pl.pallas_call(
        functools.partial(ffn_kernel, count, shape),
        out_shape=(*outs, *outs, grad_shape, grad_shape),
        in_specs=[smem, vmem] + [anywhere] * len(operands),
        out_specs=tuple([vmem] * (2 * cores + 2)),
        scratch_shapes=[
            pltpu.VMEM(token_shape, BF16),
            pltpu.VMEM(token_shape, BF16),
            pltpu.VMEM(token_shape, F32),
            pltpu.VMEM(token_shape, F32),
            pltpu.VMEM((count, col_local, slots, tile, tile), BF16),
            pltpu.VMEM((count, col_local, slots, tile, tile), BF16),
            pltpu.SemaphoreType.DMA((len(operands),)),
        ],
        compiler_params=pltpu.CompilerParams(vmem_limit_bytes=60 * 1024 * 1024),
        cost_estimate=pl.CostEstimate(
            flops=12 * count * col_local * slots * tile * tile * part_rows * cores,
            bytes_accessed=16 * 1024 * 1024,
            transcendentals=0,
        ),
    )(table, scale, *operands)
    return result[:cores], result[cores : 2 * cores], result[-2], result[-1]


def per_device(inputs, grad_out, w_up, w_down, up_rows, slot_counts, keep_mask):
    tok_dev, width_local = inputs.shape
    col_local, slots, tile, _unused = w_up.shape
    parts = lax.axis_size("tp")
    blocks = lax.axis_size("blk")
    part_rows = tok_dev // parts
    cores = 2
    chips = blocks // cores
    half = chips // 2
    shape = (cores, parts, part_rows, width_local, col_local, slots, tile)
    tp = lax.axis_index("tp")
    blk = lax.axis_index("blk")
    tie = lax.optimization_barrier

    def chip_at(pos):
        return 2 * pos if pos < half else 2 * (chips - 1 - pos) + 1

    chip, core = blk // cores, blk % cores
    ring_pos = jnp.where(chip % 2 == 0, chip // 2, chips - 1 - chip // 2)
    right, left = [], []
    for pos in range(chips):
        a, b = chip_at(pos), chip_at((pos + 1) % chips)
        for c in range(cores):
            right.append((cores * a + c, cores * b + c))
            left.append((cores * b + c, cores * a + c))
    swap = [(i, i ^ 1) for i in range(blocks)]

    def go_right(x):
        return lax.ppermute(x, "blk", right)

    def go_left(x):
        return lax.ppermute(x, "blk", left)

    def to_core(x):
        return lax.ppermute(x, "blk", swap)

    def to_part(x, k):
        return lax.ppermute(x, "tp", [(i, (i + k) % parts) for i in range(parts)])

    up, down = {0: w_up}, {0: w_down}
    if half > 1:
        for w in (up, down):
            w[-1] = go_right(w[0])
            w[1] = go_left(w[0])

    def piece(x, k):
        return lax.dynamic_slice_in_dim(x, lax.rem(tp + k, parts) * part_rows, part_rows, 0)

    x_far = [to_part(piece(inputs, k), k) for k in range(1, parts)]
    dy_far = [to_part(piece(grad_out, k), k) for k in range(1, parts)]
    x_near = to_core(piece(inputs, 0))
    dy_near = to_core(piece(grad_out, 0))

    word_count = keep_mask.shape[1]
    lanes = 128
    word_rows = cores * part_rows * word_count // lanes
    words = keep_mask.reshape(chips, cores, parts, part_rows * word_count)
    words = lax.dynamic_index_in_dim(words, tp, 2, keepdims=False)
    words = words.reshape(chips, word_rows, lanes)
    facts = jnp.concatenate([up_rows.reshape(-1), slot_counts.reshape(-1)])
    facts = jnp.pad(facts, (0, lanes - facts.shape[0])).reshape(1, 1, lanes)
    relative = jnp.arange(chips, dtype=jnp.int32)
    message = jnp.concatenate(
        [jnp.take(words, relative ^ chip, axis=0), jnp.broadcast_to(facts, (chips, 1, lanes))],
        axis=1,
    )
    bits = chips.bit_length() - 1

    def hop(message, bit):
        split = message.reshape(chips >> (bit + 1), 2, 1 << bit, word_rows + 1, lanes)
        pairs = [(i, i ^ (cores << bit)) for i in range(blocks)]
        moved = lax.ppermute(split[:, 1], "blk", pairs)
        return jnp.stack([split[:, 0], moved], axis=1).reshape(message.shape)

    bit = 0
    for step in range(1, half):
        if bit < bits:
            message = hop(message, bit)
            bit += 1
        fresh = (up[step], up[-step], down[step], down[-step], message)
        up[step], up[-step], down[step], down[-step], message = tie(fresh)
        if step + 1 < half:
            for w in (up, down):
                w[-1 - step] = go_right(w[-step])
                w[1 + step] = go_left(w[step])
        if step == max(1, half - 2):
            x_far = list(tie((message, *x_far))[1:])
            x_far_near = [to_core(x) for x in x_far]
    up[half] = go_right(up[1 - half])
    down[half] = go_left(down[half - 1])
    while bit < bits:
        message = hop(message, bit)
        bit += 1
    dy_far_near = [to_core(x) for x in dy_far]

    order = [half]
    for step in range(half - 1, 0, -1):
        order += [step, -step]
    order.append(0)

    owner_pos = lax.rem(ring_pos + jnp.asarray(order, jnp.int32) + chips, chips)
    owner_chip = jnp.where(owner_pos < half, 2 * owner_pos, 2 * (chips - 1 - owner_pos) + 1)
    rel = owner_chip ^ chip
    table = jnp.take(message[:, word_rows, : col_local * (slots + 1)], rel, axis=0)
    table = jnp.concatenate([table, rel[:, None]], axis=1)
    table = jnp.concatenate([table, jnp.full((1, table.shape[1]), tp, jnp.int32)], axis=0)

    columns = jnp.arange(col_local * tile, dtype=jnp.int32)
    token_words = message[:, :word_rows].reshape(chips * cores * part_rows, word_count)
    picked = jnp.take(token_words, columns // 16, axis=1)
    keep = jnp.bitwise_and(jnp.right_shift(picked, columns % 16), 1)
    scale = (keep.astype(F32) * KEEP_SCALE).astype(BF16)
    scale = scale.reshape(chips, cores, part_rows, col_local * tile)
    scale = jnp.where(core == 0, scale, scale[:, ::-1])
    scale = scale.reshape(chips, cores * part_rows, col_local * tile)

    outs, gins, gup, gdown = run_ffn(
        table,
        scale,
        [inputs, *x_far, x_near, *x_far_near],
        [grad_out, *dy_far, dy_near, *dy_far_near],
        [up[d] for d in order],
        [down[d] for d in order],
        shape,
    )

    def term(grads, d):
        return grads[order.index(d)]

    moving = {
        "up_right": go_right(term(gup, half).astype(BF16)),
        "down_left": go_left(term(gdown, half).astype(BF16)),
    }

    def finish(pair):
        own, other = pair
        return (own + to_core(other).astype(F32)).astype(BF16)

    sums = (finish(outs), finish(gins))
    sums, moving = tie((sums, moving))

    def to_width(total):
        kept = lax.dynamic_index_in_dim(total, tp, 0, keepdims=False)
        sent = [
            to_part(lax.dynamic_index_in_dim(total, lax.rem(tp + k, parts), 0, keepdims=False), k)
            for k in range(1, parts)
        ]
        return [kept, *sent]

    arrived = (to_width(sums[0]), to_width(sums[1]))
    for step in range(half - 1, 0, -1):
        later = {}
        for name, grads in (("up", gup), ("down", gdown)):
            for side, sign, go in (("right", 1, go_right), ("left", -1, go_left)):
                key = f"{name}_{side}"
                value = term(grads, sign * step)
                if key in moving:
                    value = value + moving[key].astype(F32)
                later[key] = go(value.astype(BF16))
        moving = later

    def total_of(name, grads):
        total = term(grads, 0)
        for side in ("right", "left"):
            if f"{name}_{side}" in moving:
                total = total + moving[f"{name}_{side}"].astype(F32)
        return total

    totals = (total_of("up", gup), total_of("down", gdown))
    totals, arrived = tie((totals, arrived))

    rows = tile // parts
    live = jnp.arange(slots, dtype=jnp.int32)[None, :] < slot_counts[:, None]

    def reduce_tp(total):
        out = lax.dynamic_slice_in_dim(total, tp * rows, rows, 2)
        for k in range(1, parts):
            dest = lax.rem(tp + k, parts)
            moved = to_part(lax.dynamic_slice_in_dim(total, dest * rows, rows, 2), k)
            out = out + moved
        return jnp.where(live[:, :, None, None], out, 0.0).astype(BF16)

    grad_up, grad_down = reduce_tp(totals[0]), reduce_tp(totals[1])

    def assemble(arrived):
        place = lax.broadcasted_iota(jnp.int32, (parts, 1, 1), 0)
        out = arrived[0][None]
        for k in range(1, parts):
            out = jnp.where(place == lax.rem(tp + parts - k, parts), arrived[k][None], out)
        return out.reshape(tok_dev, width_local)

    return (assemble(arrived[0]), assemble(arrived[1]), grad_up, grad_down)


def solution(mesh):
    return jax.shard_map(
        per_device,
        mesh=mesh,
        in_specs=(
            P("blk", "tp"),
            P("blk", "tp"),
            P("blk", None, None, None),
            P("blk", None, None, None),
            P("blk", None),
            P("blk"),
            P(None, "blk"),
        ),
        out_specs=(
            P("blk", "tp"),
            P("blk", "tp"),
            P("blk", None, "tp", None),
            P("blk", None, "tp", None),
        ),
        check_vma=False,
    )
```

```python
import functools

import jax
import jax.numpy as jnp
from jax import lax
from jax.experimental import pallas as pl
from jax.experimental.pallas import tpu as pltpu
from jax.sharding import PartitionSpec as P

INV_ROOT_TWO = 0.7071067811865476
INV_ROOT_TAU = 0.3989422804014327
KEEP_SCALE = 1.25
F32 = jnp.float32
BF16 = jnp.bfloat16


def mm(a, b, dims):
    return lax.dot_general(a, b, (dims, ((), ())), preferred_element_type=F32)


def ffn_kernel(count, shape, fact_ref, rel_ref, word_ref, *refs):
    cores, parts, part_rows, width_local, col_local, slots, tile, word_count = shape
    tokens = cores * part_rows
    hidden_local = col_local * tile
    refs = list(refs)

    def take(number):
        out = refs[:number]
        del refs[:number]
        return out

    xs_refs = take(cores * parts)
    dys_refs = take(cores * parts)
    far_refs = take(2)
    near_refs = take(count - 1)
    own_ref, other_ref, far_up_ref, far_down_ref, grad_ref = take(5)
    (other_acc,) = take(1)
    accs = (own_ref, other_acc)

    me = rel_ref[count]
    mine = pl.ds(pl.multiple_of(me * part_rows, part_rows), part_rows)

    def columns(pieces, row):
        part = lax.div(row, row_local)
        lane = pl.ds(pl.multiple_of(lax.rem(row, row_local) * tile, tile), tile)
        halves = []
        for core in range(cores):
            value = None
            for k in range(parts):
                ref = pieces[core * parts + k]
                got = ref[mine, lane] if core == 0 and k == 0 else ref[:, lane]
                here = part == lax.rem(me + parts - k, parts)
                value = got if value is None else jnp.where(here, got, value)
            halves.append(value)
        return jnp.concatenate(halves, axis=0)

    def weight(k, which, c, s):
        return far_refs[which][c, s] if k == 0 else near_refs[k - 1][which, c, s]

    for acc in accs:
        acc[...] = jnp.zeros_like(acc)
    unit = lax.broadcasted_iota(jnp.int32, (2 * word_count, hidden_local), 1)
    source = lax.broadcasted_iota(jnp.int32, (2 * word_count, hidden_local), 0)
    wanted = lax.div(unit, 16) + word_count * lax.div(lax.rem(unit, 16), 8)
    pick = jnp.where(source == wanted, 1.0, 0.0).astype(BF16)
    bit_of = lax.rem(lax.broadcasted_iota(jnp.int32, (tokens, hidden_local), 1), 8)
    row_local = width_local // tile
    per_step = 2

    for step in range(0, count, per_step):
        items = []
        for k in range(step, min(step + per_step, count)):
            pos = rel_ref[k]
            words = word_ref[pos, :word_count, :]
            low, high = jnp.bitwise_and(words, 255), jnp.right_shift(words, 8)
            octets = jnp.concatenate([low, high], axis=0).astype(F32).astype(BF16)
            chosen = mm(octets, pick, ((0,), (0,))).astype(jnp.int32)
            keep = jnp.bitwise_and(jnp.right_shift(chosen, bit_of), 1)
            scales = keep.astype(F32) * KEEP_SCALE
            for c in range(col_local):
                lives = fact_ref[pos, col_local * slots + c]
                where, xs, dys, ups, downs = [], [], [], [], []
                for s in range(slots):
                    row = fact_ref[pos, c * slots + s]
                    lane = pl.multiple_of(lax.rem(row, row_local) * tile, tile)
                    where.append((lax.div(row, row_local), lane))
                    xs.append(columns(xs_refs, row))
                    dys.append(columns(dys_refs, row))
                    zero = jnp.zeros((tile, tile), BF16)
                    ups.append(jnp.where(s < lives, weight(k, 0, c, s), zero))
                    downs.append(jnp.where(s < lives, weight(k, 1, c, s), zero))
                pre = mm(xs[0], ups[0], ((1,), (0,)))
                grad_hidden = mm(dys[0], downs[0], ((1,), (1,)))
                for s in range(1, slots):
                    pre += mm(xs[s], ups[s], ((1,), (0,)))
                    grad_hidden += mm(dys[s], downs[s], ((1,), (1,)))
                scale = scales[:, c * tile : (c + 1) * tile]
                items.append((k, c, scale, where, xs, dys, ups, downs, pre, grad_hidden))
        ready = []
        for k, c, scale, where, xs, dys, ups, downs, pre, grad_hidden in items:
            phi = 0.5 * (1.0 + lax.erf(pre * INV_ROOT_TWO))
            slope = phi + pre * jnp.exp(-0.5 * pre * pre) * INV_ROOT_TAU
            hidden = (pre * phi * scale).astype(BF16)
            grad_pre = (grad_hidden * scale * slope).astype(BF16)
            ready.append((k, c, where, xs, dys, ups, downs, hidden, grad_pre))
        for k, c, where, xs, dys, ups, downs, hidden, grad_pre in ready:
            for s in range(slots):
                grad_ref[k, 0, c, s] = mm(xs[s], grad_pre, ((0,), (0,)))
                grad_ref[k, 1, c, s] = mm(hidden, dys[s], ((0,), (0,)))
        for k, c, where, xs, dys, ups, downs, hidden, grad_pre in ready:
            for s, (p, o) in enumerate(where):
                out_term = mm(hidden, downs[s], ((1,), (0,)))
                in_term = mm(grad_pre, ups[s], ((1,), (1,)))
                for core, acc in enumerate(accs):
                    at = slice(core * part_rows, (core + 1) * part_rows)
                    acc[0, p, :, pl.ds(o, tile)] += out_term[at]
                    acc[1, p, :, pl.ds(o, tile)] += in_term[at]
    far_up_ref[...] = grad_ref[0, 0].astype(BF16)
    far_down_ref[...] = grad_ref[0, 1].astype(BF16)
    other_ref[...] = other_acc[...].astype(BF16)


def run_ffn(facts, rels, words, xs, dys, far, near, shape):
    cores, parts, part_rows, width_local, col_local, slots, tile, _words = shape
    count = len(near) + 1
    vmem = pl.BlockSpec(memory_space=pltpu.VMEM)
    smem = pl.BlockSpec(memory_space=pltpu.SMEM)
    part_shape = (2, parts, part_rows, width_local)
    tiles_shape = (col_local, slots, tile, tile)
    operands = [pltpu.with_memory_space_constraint(x, pltpu.VMEM) for x in [words, *xs, *dys, *far, *near]]
    return pl.pallas_call(
        functools.partial(ffn_kernel, count, shape),
        out_shape=(
            pltpu.VMEM(part_shape, F32),
            pltpu.VMEM(part_shape, BF16),
            pltpu.VMEM(tiles_shape, BF16),
            pltpu.VMEM(tiles_shape, BF16),
            pltpu.VMEM((count, 2, *tiles_shape), F32),
        ),
        in_specs=[smem, smem] + [vmem] * len(operands),
        out_specs=tuple([vmem] * 5),
        scratch_shapes=[pltpu.VMEM(part_shape, F32)],
        compiler_params=pltpu.CompilerParams(vmem_limit_bytes=12 * 1024 * 1024),
        cost_estimate=pl.CostEstimate(
            flops=12 * count * col_local * slots * tile * tile * part_rows * cores,
            bytes_accessed=16 * 1024 * 1024,
            transcendentals=0,
        ),
    )(facts, rels, *operands)


def per_device(inputs, grad_out, w_up, w_down, up_rows, slot_counts, keep_mask):
    tok_dev, width_local = inputs.shape
    col_local, slots, tile, _unused = w_up.shape
    parts = lax.axis_size("tp")
    blocks = lax.axis_size("blk")
    part_rows = tok_dev // parts
    cores = 2
    chips = blocks // cores
    half = chips // 2
    word_count = keep_mask.shape[1]
    tokens = cores * part_rows
    shape = (cores, parts, part_rows, width_local, col_local, slots, tile, word_count)
    tp = lax.axis_index("tp")
    blk = lax.axis_index("blk")
    tie = lax.optimization_barrier

    def chip_at(pos):
        return 2 * pos if pos < half else 2 * (chips - 1 - pos) + 1

    chip, core = blk // cores, blk % cores
    ring_pos = jnp.where(chip % 2 == 0, chip // 2, chips - 1 - chip // 2)
    right, left = [], []
    for pos in range(chips):
        a, b = chip_at(pos), chip_at((pos + 1) % chips)
        for c in range(cores):
            right.append((cores * a + c, cores * b + c))
            left.append((cores * b + c, cores * a + c))
    swap = [(i, i ^ 1) for i in range(blocks)]

    def go_right(x):
        return lax.ppermute(x, "blk", right)

    def go_left(x):
        return lax.ppermute(x, "blk", left)

    def to_core(x):
        return lax.ppermute(x, "blk", swap)

    def to_part(x, k):
        return lax.ppermute(x, "tp", [(i, (i + k) % parts) for i in range(parts)])

    w = {0: jnp.stack([w_up, w_down])}
    if half > 1:
        w[-1], w[1] = go_right(w[0]), go_left(w[0])

    def piece(x, k):
        return lax.dynamic_slice_in_dim(x, lax.rem(tp + k, parts) * part_rows, part_rows, 0)

    x_far = [to_part(piece(inputs, k), k) for k in range(1, parts)]
    dy_far = [to_part(piece(grad_out, k), k) for k in range(1, parts)]
    x_near = to_core(piece(inputs, 0))
    dy_near = to_core(piece(grad_out, 0))

    words = keep_mask.reshape(chips, cores, parts, part_rows, word_count)
    words = lax.dynamic_index_in_dim(words, tp, 2, keepdims=False)
    words = jnp.where(core == 0, words, words[:, ::-1])
    words = words.reshape(chips, tokens, word_count).transpose(0, 2, 1)
    facts = jnp.concatenate([up_rows.reshape(-1), slot_counts.reshape(-1)])
    fact_count = facts.shape[0]
    facts = jnp.pad(facts, (0, tokens - fact_count)).reshape(1, 1, tokens)
    relative = jnp.arange(chips, dtype=jnp.int32)
    message = jnp.concatenate(
        [jnp.take(words, relative ^ chip, axis=0), jnp.broadcast_to(facts, (chips, 1, tokens))],
        axis=1,
    )
    bits = chips.bit_length() - 1

    def hop(message, bit):
        split = message.reshape(chips >> (bit + 1), 2, 1 << bit, word_count + 1, tokens)
        pairs = [(i, i ^ (cores << bit)) for i in range(blocks)]
        moved = lax.ppermute(split[:, 1], "blk", pairs)
        return jnp.stack([split[:, 0], moved], axis=1).reshape(message.shape)

    bit = 0
    for step in range(1, half):
        if bit < bits:
            message = hop(message, bit)
            bit += 1
        w[step], w[-step], message = tie((w[step], w[-step], message))
        if step + 1 < half:
            w[-1 - step], w[1 + step] = go_right(w[-step]), go_left(w[step])
        if step == max(1, half - 2):
            x_far = list(tie((message, *x_far))[1:])
            x_far_near = [to_core(x) for x in x_far]
    far = [go_right(w[1 - half][0]), go_left(w[half - 1][1])]
    while bit < bits:
        message = hop(message, bit)
        bit += 1
    dy_far_near = [to_core(x) for x in dy_far]

    order = [half]
    for step in range(half - 1, 0, -1):
        order += [step, -step]
    order.append(0)
    owner_pos = lax.rem(ring_pos + jnp.asarray(order, jnp.int32) + chips, chips)
    owner_chip = jnp.where(owner_pos < half, 2 * owner_pos, 2 * (chips - 1 - owner_pos) + 1)
    rels = jnp.concatenate([owner_chip ^ chip, tp[None]])

    own, other, far_up, far_down, grads = run_ffn(
        message[:, word_count, :fact_count],
        rels,
        message,
        [inputs, *x_far, x_near, *x_far_near],
        [grad_out, *dy_far, dy_near, *dy_far_near],
        far,
        [w[d] for d in order[1:]],
        shape,
    )

    moved_up, moved_down = go_right(far_up), go_left(far_down)
    from_core = to_core(other)

    def part_of(k):
        at = lax.rem(tp + k, parts)
        a = lax.dynamic_index_in_dim(own, at, 1, keepdims=False)
        b = lax.dynamic_index_in_dim(from_core, at, 1, keepdims=False)
        return (a + b.astype(F32)).astype(BF16)

    pieces = [part_of(k) for k in range(1, parts)]
    pieces, moved_up, moved_down = tie((pieces, moved_up, moved_down))
    arrived = [to_part(x, k + 1) for k, x in enumerate(pieces)]

    zero = jnp.zeros((), F32)
    extra_right = jnp.stack([moved_up.astype(F32), jnp.broadcast_to(zero, moved_up.shape)])
    extra_left = jnp.stack([jnp.broadcast_to(zero, moved_down.shape), moved_down.astype(F32)])
    for step in range(half - 1, 0, -1):
        value_right = grads[order.index(step)] + extra_right
        value_left = grads[order.index(-step)] + extra_left
        extra_right = go_right(value_right.astype(BF16)).astype(F32)
        extra_left = go_left(value_left.astype(BF16)).astype(F32)
    total = grads[order.index(0)] + extra_right + extra_left
    total, arrived = tie((total, arrived))

    rows = tile // parts
    live = jnp.arange(slots, dtype=jnp.int32)[None, :] < slot_counts[:, None]
    summed = lax.dynamic_slice_in_dim(total, tp * rows, rows, 3)
    for k in range(1, parts):
        at = lax.rem(tp + k, parts) * rows
        summed = summed + to_part(lax.dynamic_slice_in_dim(total, at, rows, 3), k)
    summed = jnp.where(live[None, :, :, None, None], summed, 0.0).astype(BF16)

    place = lax.broadcasted_iota(jnp.int32, (parts, 1, 1), 0)
    kept = part_of(0)
    results = []
    for which in range(2):
        out = kept[which][None]
        for k in range(1, parts):
            here = place == lax.rem(tp + parts - k, parts)
            out = jnp.where(here, arrived[k - 1][which][None], out)
        results.append(out.reshape(tok_dev, width_local))

    return (results[0], results[1], summed[0], summed[1])


def solution(mesh):
    return jax.shard_map(
        per_device,
        mesh=mesh,
        in_specs=(
            P("blk", "tp"),
            P("blk", "tp"),
            P("blk", None, None, None),
            P("blk", None, None, None),
            P("blk", None),
            P("blk"),
            P(None, "blk"),
        ),
        out_specs=(
            P("blk", "tp"),
            P("blk", "tp"),
            P("blk", None, "tp", None),
            P("blk", None, "tp", None),
        ),
        check_vma=False,
    )
```
